128 devices in a mesh: sector: 8 (over z, core), mode: 16 (over y, x).
Axes of the slice: x: 4, y: 4, z: 4, core: 2. Of those that a mesh axis runs over, the one named last changes fastest.
Arguments:
- modes: bfloat16 [256, 3, 32, 80, 128], P('mode', None, 'sector'), may hold values from -0.1875 to 0.1875
- thickness: float32 [32, 80, 128], P('sector'), may hold values from -6 to 6
- stiff_taps: float32 [27], replicated, may hold values from -1.25 to 1.25
- mass_taps: float32 [27], replicated, may hold values from 0.02 to 0.2
- eigenvalues: float32 [256], P('mode'), may hold values from 0.5 to 2
Outputs:
- sensitivity: float32 [256, 256], P('sector', 'mode')
The draws below stay inside these ranges and needn't reach their ends.
All inputs are finite; a program needn't handle non-finite values.
Results may differ from the reference program's by a relative error of at most 0.0029.
Values may be sent and summed in bfloat16 or wider, within the bound.
A program may use at most 64 MiB of HBM per device.

```python
import math
import jax
import jax.numpy as jnp
from jax import lax

MODES = 256
COMP = 3
NY = 80
NZ = 128
NX = 32


def levels(rng, dims, split, smallest, top_value):
    def one(position, shards_of):
        steps = jax.random.uniform(jax.random.fold_in(jax.random.fold_in(rng, 6), position), (shards_of,), jnp.float32, smallest / len(split), top_value / len(split))
        return jnp.repeat(jnp.exp(steps), dims[position] // shards_of).reshape((-1,) + (1,) * (len(dims) - position - 1))

    loudness = one(*split[0])
    for cut in split[1:]:
        loudness = loudness * one(*cut)
    return loudness


def bell_draw(key, dims, scale, reach, pieces=(), dtype=jnp.bfloat16):
    array = scale * jax.random.normal(key, dims, jnp.float32)
    if pieces:
        array = array * levels(key, dims, pieces, -0.22, 0.18)
    return jnp.clip(array, -reach, reach).astype(dtype)


def setup_inputs(seed: int = 0) -> dict:
    keys = jax.random.split(jax.random.key(seed), 6)
    return {
        "modes": bell_draw(keys[0], (MODES, COMP, NX, NY, NZ), ((COMP * NX * NY * NZ) ** -0.25), 0.1875, ((0, 16), (2, 8))),
        "thickness": bell_draw(keys[1], (NX, NY, NZ), 1.0, 6.0, ((0, 8),), jnp.float32),
        "stiff_taps": bell_draw(keys[2], (27,), 0.2, 1.25, (), jnp.float32),
        "mass_taps": jnp.clip(jnp.exp(jax.random.uniform(keys[3], (27,), jnp.float32, math.log(0.02), math.log(0.2))), 0.02, 0.2),
        "eigenvalues": jnp.clip(jnp.exp(math.log(2.0) - 1.3862944 * jax.random.uniform(keys[4], (MODES,), jnp.float32) ** levels(keys[4], (MODES,), ((0, 16),), -0.2, 0.2)), 0.5, 2.0),
    }


def load_block(block, lams, padded_thick, stiff_taps, mass_taps):
    field = jnp.pad(block.astype(jnp.float32), ((0, 0), (0, 0), (1, 1), (1, 1), (1, 1)))
    sx = field.shape[2] - 2
    sy = field.shape[3] - 2
    sz = field.shape[4] - 2
    centre = padded_thick[1:1 + sx, 1:1 + sy, 1:1 + sz]
    stiff_acc = jnp.zeros(block.shape, jnp.float32)
    mass_acc = jnp.zeros(block.shape, jnp.float32)
    for aoff in range(3):
        for boff in range(3):
            for doff in range(3):
                index = 9 * aoff + 3 * boff + doff
                coeff = 0.5 * (centre + padded_thick[aoff:aoff + sx, boff:boff + sy, doff:doff + sz])
                moved = coeff * field[:, :, aoff:aoff + sx, boff:boff + sy, doff:doff + sz]
                stiff_acc = stiff_acc + stiff_taps[index] * moved
                mass_acc = mass_acc + mass_taps[index] * moved
    loaded = stiff_acc - lams[:, None, None, None, None] * mass_acc
    return loaded.astype(jnp.bfloat16)


def reference(modes, thickness, stiff_taps, mass_taps, eigenvalues):
    padded_thick = jnp.pad(thickness, 1)
    count = modes.shape[0] // 16
    blocks = modes.reshape((count, 16) + modes.shape[1:])
    lam_blocks = eigenvalues.reshape(count, 16)
    loaded = lax.map(lambda pair: load_block(pair[0], pair[1], padded_thick, stiff_taps, mass_taps), (blocks, lam_blocks))
    loaded = loaded.reshape(modes.shape[0], -1)
    return jnp.dot(modes.reshape(modes.shape[0], -1), loaded.T, preferred_element_type=jnp.float32)
```

```python
import functools

import jax
import jax.numpy as jnp
from jax import lax
from jax.experimental import pallas as pl
from jax.experimental.pallas import tpu as pltpu
from jax.sharding import PartitionSpec as P

MESH = pl.DeviceIdType.MESH
GROUPS = 16
SECTORS = 8
OWN = 15
ROWS = 16
PLANES = 4
NZ = 128
MODES = 256
NY = 80
ALL_ROWS = 240
PIECES = ((0, 0, 16), (1, 0, 16), (2, 0, 16), (3, 0, 4), (3, 4, 4), (3, 8, 4), (3, 12, 4))


def kernel(
    src, thick, stiff, mass, eig, out,
    m, images, thk, trow, tcol, taps, lamb, acc, sums, parts, blocks,
    send_sem, recv_sem, own_sem, rim_sem, thick_sem, lam_send, lam_recv, sum_send, sum_recv, blk_send, blk_recv,
):
    sec = lax.axis_index("sector")
    me = lax.axis_index("mode")
    me_x = lax.rem(me, 4)
    me_y = lax.div(me, 4)
    before = lax.rem(sec + SECTORS - 1, SECTORS)

    def peer(off):
        dx = lax.rem(off, 4)
        dy = lax.div(off, 4)
        return lax.rem(me_y + dy, 4) * 4 + lax.rem(me_x + dx, 4)

    def first_row(group):
        return jnp.minimum(group * OWN, ALL_ROWS - ROWS)

    m[:, :, ROWS] = jnp.zeros((PLANES + 1, GROUPS, 16, NZ), jnp.bfloat16)
    barrier = pltpu.get_barrier_semaphore()

    @pl.loop(1, GROUPS)
    def _(off):
        pl.semaphore_signal(barrier, inc=1, device_id=(sec, peer(off)), device_id_type=MESH)

    @pl.loop(1, SECTORS)
    def _(off):
        pl.semaphore_signal(
            barrier, inc=1, device_id=(lax.rem(sec + off, SECTORS), me), device_id_type=MESH
        )

    own_first = first_row(me)
    own = [
        pltpu.make_async_copy(
            src.at[plane, pl.ds(own_first, ROWS)], m.at[plane, me, pl.ds(0, ROWS)], own_sem.at[plane]
        )
        for plane in range(PLANES)
    ]
    for copy in own:
        copy.start()
    for j in range(GROUPS):
        lamb[me, j : j + 1, :] = jnp.full((1, NZ), eig[j], jnp.float32)
    pl.semaphore_wait(barrier, GROUPS - 1 + SECTORS - 1)

    def piece_copy(index, dest, origin):
        plane, row, rows = PIECES[index]
        return pltpu.make_async_remote_copy(
            src_ref=src.at[plane, pl.ds(first_row(dest) + row, rows)],
            dst_ref=m.at[plane, origin, pl.ds(row, rows)],
            send_sem=send_sem.at[index, dest],
            recv_sem=recv_sem.at[index, origin],
            device_id=(sec, dest),
            device_id_type=MESH,
        )

    def lam_copy(dest, origin):
        return pltpu.make_async_remote_copy(
            src_ref=lamb.at[me],
            dst_ref=lamb.at[origin],
            send_sem=lam_send.at[dest],
            recv_sem=lam_recv.at[origin],
            device_id=(sec, dest),
            device_id_type=MESH,
        )

    thick_copy = pltpu.make_async_remote_copy(
        src_ref=thick.at[0],
        dst_ref=thk,
        send_sem=thick_sem.at[0],
        recv_sem=thick_sem.at[1],
        device_id=(before, me),
        device_id_type=MESH,
    )
    thick_copy.start()
    for index in range(len(PIECES)):

        @pl.loop(1, GROUPS)
        def _(off, index=index):
            piece_copy(index, peer(off), me).start()

        if index == 0:

            @pl.loop(1, GROUPS)
            def _(off):
                lam_copy(peer(off), me).start()

    acc[...] = jnp.zeros_like(acc)
    tcol[:, ROWS] = jnp.zeros((PLANES + 1, NZ, NZ), jnp.float32)
    diff = lax.broadcasted_iota(jnp.int32, (NZ, NZ), 0) - lax.broadcasted_iota(
        jnp.int32, (NZ, NZ), 1
    )
    for ab in range(9):
        for half, table in enumerate((stiff, mass)):
            value = jnp.where(
                diff == 0,
                table[3 * ab + 1],
                jnp.where(
                    diff == 1,
                    table[3 * ab + 2],
                    jnp.where(diff == -1, table[3 * ab], 0.0),
                ),
            )
            taps[ab, :, half * NZ : (half + 1) * NZ] = 0.5 * value

    def thick_rows(plane, ref):
        @pl.loop(0, ROWS)
        def _(l):
            y = lax.rem(own_first + l, NY)
            trow[plane, pl.ds(l, 1), :] = ref[pl.ds(y, 1), :]

        column = jnp.transpose(trow[plane])
        for l in range(ROWS):
            tcol[plane, l] = jnp.broadcast_to(column[:, l : l + 1], (NZ, NZ))

    trow[...] = jnp.zeros_like(trow)
    for plane in range(PLANES):
        thick_rows(plane, thick.at[plane])
    thick_copy.wait()
    thick_rows(PLANES, thk)

    last_group = me == GROUPS - 1
    end_sector = sec == SECTORS - 1

    def source_row(l, b, cross_end):
        if b == 0:
            ok = jnp.where(last_group, l >= 1, l < ROWS - 1)
        else:
            low = l if b == 1 else l - 1
            ok = jnp.where(last_group, low >= 1, low >= 0) & (low < ROWS - 1)
            ok = ok & (lax.rem(own_first + low + 1, NY) != 0)
        if cross_end:
            ok = ok & jnp.logical_not(end_sector)
        return jnp.where(ok, l + b, ROWS)

    def image_of(l, plane_out, plane):
        centre = trow[plane_out, pl.ds(l, 1), :]
        fields, highs, lows = [], [], []
        for b in (-1, 0, 1):
            r = source_row(l, b, max(plane, plane_out) == PLANES)
            ab = 3 * (plane - plane_out + 1) + b + 1
            fields.append(m[plane, :, r].reshape(MODES, NZ))
            both = centre + tcol[plane, r]
            coeff = jnp.concatenate([both, both], axis=1) * taps[ab]
            high = coeff.astype(jnp.bfloat16)
            highs.append(high)
            lows.append((coeff - high.astype(jnp.float32)).astype(jnp.bfloat16))
        return jnp.dot(
            jnp.concatenate(fields + fields, axis=1),
            jnp.concatenate(highs + lows, axis=0),
            preferred_element_type=jnp.float32,
        )

    def row_step(l, plane, outs):
        loads, rows = [], []
        for plane_out, begun, complete in outs:
            image = image_of(l, plane_out, plane)
            if not begun:
                image = image + images[plane_out, l]
            if not complete:
                images[plane_out, l] = image
                continue
            lam = lamb[...].reshape(MODES, NZ)
            loads.append((image[:, :NZ] - lam * image[:, NZ:]).astype(jnp.bfloat16))
            rows.append(m[plane_out, :, l].reshape(MODES, NZ))
        if loads:
            gram = lax.dot_general(
                jnp.concatenate(loads, axis=1),
                jnp.concatenate(rows, axis=1),
                (((1,), (1,)), ((), ())),
                preferred_element_type=jnp.float32,
            )
            acc[...] += gram.reshape(GROUPS, 16, MODES)

    def process(plane, outs, low, high):
        @pl.loop(low, high)
        def _(l):
            row_step(l, plane, outs)

    def arrived(index):
        @pl.loop(1, GROUPS)
        def _(off):
            piece_copy(index, me, peer(off)).wait_recv()

    arrived(0)
    own[0].wait()
    rim = pltpu.make_async_remote_copy(
        src_ref=m.at[0],
        dst_ref=m.at[PLANES],
        send_sem=rim_sem.at[0],
        recv_sem=rim_sem.at[1],
        device_id=(before, me),
        device_id_type=MESH,
    )
    rim.start()

    @pl.loop(1, GROUPS)
    def _(off):
        lam_copy(me, peer(off)).wait_recv()

    process(0, [(0, True, False), (1, True, False)], 0, ROWS)
    arrived(1)
    own[1].wait()
    process(1, [(0, False, True), (1, False, False), (2, True, False)], 0, ROWS)
    arrived(2)
    own[2].wait()
    process(2, [(1, False, True), (2, False, False), (3, True, False)], 0, ROWS)
    rim.wait()
    process(4, [(3, False, False)], 0, ROWS)
    own[3].wait()
    for quarter in range(4):
        arrived(3 + quarter)
        process(
            3,
            [(2, False, True), (3, False, True), (4, True, True)],
            max(0, 4 * quarter - 1),
            ROWS if quarter == 3 else 4 * quarter + 3,
        )

    def sum_copy(dest, origin):
        return pltpu.make_async_remote_copy(
            src_ref=acc.at[dest],
            dst_ref=sums.at[origin],
            send_sem=sum_send.at[dest],
            recv_sem=sum_recv.at[origin],
            device_id=(sec, dest),
            device_id_type=MESH,
        )

    @pl.loop(1, GROUPS)
    def _(off):
        sum_copy(peer(off), me).start()

    sums[me] = acc[me]

    @pl.loop(1, GROUPS)
    def _(off):
        sum_copy(me, peer(off)).wait_recv()

    total = sums[0]
    for p in range(1, GROUPS):
        total = total + sums[p]
    for s in range(SECTORS):
        parts[s, :, 0:32] = total[:, 32 * s : 32 * s + 32]
        parts[s, :, 32:NZ] = jnp.zeros((16, NZ - 32), jnp.float32)

    def block_copy(dest, origin):
        return pltpu.make_async_remote_copy(
            src_ref=parts.at[dest],
            dst_ref=blocks.at[origin],
            send_sem=blk_send.at[dest],
            recv_sem=blk_recv.at[origin],
            device_id=(dest, me),
            device_id_type=MESH,
        )

    @pl.loop(1, SECTORS)
    def _(off):
        block_copy(lax.rem(sec + off, SECTORS), sec).start()

    blocks[sec] = parts[sec]

    @pl.loop(1, SECTORS)
    def _(off):
        block_copy(sec, lax.rem(sec + off, SECTORS)).wait_recv()

    block = blocks[0]
    for s in range(1, SECTORS):
        block = block + blocks[s]
    out[...] = jnp.transpose(block)[0:32, :]

    for index in range(len(PIECES)):

        @pl.loop(1, GROUPS)
        def _(off, index=index):
            piece_copy(index, peer(off), me).wait_send()

    @pl.loop(1, GROUPS)
    def _(off):
        lam_copy(peer(off), me).wait_send()
        sum_copy(peer(off), me).wait_send()

    @pl.loop(1, SECTORS)
    def _(off):
        block_copy(lax.rem(sec + off, SECTORS), sec).wait_send()


def on_device(modes, thickness, stiff_taps, mass_taps, eigenvalues):
    src = modes.transpose(2, 1, 3, 0, 4).reshape(PLANES, ALL_ROWS, 16, NZ)
    smem = pl.BlockSpec(memory_space=pltpu.SMEM)
    vmem = pl.BlockSpec(memory_space=pltpu.VMEM)
    dma = pltpu.SemaphoreType.DMA
    f32 = jnp.float32
    return pl.pallas_call(
        kernel,
        out_shape=jax.ShapeDtypeStruct((32, 16), f32),
        in_specs=[pl.BlockSpec(memory_space=pl.ANY), vmem, smem, smem, smem],
        out_specs=vmem,
        scratch_shapes=[
            pltpu.VMEM((PLANES + 1, GROUPS, ROWS + 1, 16, NZ), jnp.bfloat16),
            pltpu.VMEM((PLANES, ROWS, MODES, 2 * NZ), f32),
            pltpu.VMEM((NY, NZ), f32),
            pltpu.VMEM((PLANES + 1, NZ, NZ), f32),
            pltpu.VMEM((PLANES + 1, ROWS + 1, NZ, NZ), f32),
            pltpu.VMEM((9, NZ, 2 * NZ), f32),
            pltpu.VMEM((GROUPS, 16, NZ), f32),
            pltpu.VMEM((GROUPS, 16, MODES), f32),
            pltpu.VMEM((GROUPS, 16, MODES), f32),
            pltpu.VMEM((SECTORS, 16, NZ), f32),
            pltpu.VMEM((SECTORS, 16, NZ), f32),
            dma((len(PIECES), GROUPS)),
            dma((len(PIECES), GROUPS)),
            dma((PLANES,)),
            dma((2,)),
            dma((2,)),
            dma((GROUPS,)),
            dma((GROUPS,)),
            dma((GROUPS,)),
            dma((GROUPS,)),
            dma((SECTORS,)),
            dma((SECTORS,)),
        ],
        compiler_params=pltpu.CompilerParams(
            collective_id=0, has_side_effects=True, vmem_limit_bytes=48 * 2**20
        ),
    )(src, thickness, stiff_taps, mass_taps, eigenvalues)


def solution(mesh):
    in_specs = (P("mode", None, "sector", None, None), P("sector", None, None), P(), P(), P("mode"))
    return jax.shard_map(
        on_device, mesh=mesh, in_specs=in_specs, out_specs=P("sector", "mode"), check_vma=False
    )
```

```python
import functools

import jax
import jax.numpy as jnp
from jax import lax
from jax.experimental import pallas as pl
from jax.experimental.pallas import tpu as pltpu
from jax.sharding import PartitionSpec as P

MESH = pl.DeviceIdType.MESH
GROUPS = 16
SECTORS = 8
OWN = 15
ROWS = 16
PLANES = 4
NZ = 128
MODES = 256
NY = 80
ALL_ROWS = 240
PIECES = ((0, 0, 16), (1, 0, 16), (2, 0, 16), (3, 0, 8), (3, 8, 4), (3, 12, 4))


def kernel(
    src, thick, stiff, mass, eig, out,
    m, images, matrix, single, coeffs, bands, thk, trow, lamb, acc, sums, parts, blocks,
    send_sem, recv_sem, own_sem, rim_sem, thick_sem, lam_send, lam_recv, sum_send, sum_recv, blk_send, blk_recv,
):
    sec = lax.axis_index("sector")
    me = lax.axis_index("mode")
    me_x = lax.rem(me, 4)
    me_y = lax.div(me, 4)
    before = lax.rem(sec + SECTORS - 1, SECTORS)

    def peer(off):
        dx = lax.rem(off, 4)
        dy = lax.div(off, 4)
        return lax.rem(me_y + dy, 4) * 4 + lax.rem(me_x + dx, 4)

    def first_row(group):
        return jnp.minimum(group * OWN, ALL_ROWS - ROWS)

    m[:, :, ROWS] = jnp.zeros((PLANES + 1, GROUPS, 16, NZ), jnp.bfloat16)
    barrier = pltpu.get_barrier_semaphore()

    @pl.loop(1, GROUPS)
    def _(off):
        pl.semaphore_signal(barrier, inc=1, device_id=(sec, peer(off)), device_id_type=MESH)

    @pl.loop(1, SECTORS)
    def _(off):
        pl.semaphore_signal(
            barrier, inc=1, device_id=(lax.rem(sec + off, SECTORS), me), device_id_type=MESH
        )

    own_first = first_row(me)
    own = [
        pltpu.make_async_copy(
            src.at[plane, pl.ds(own_first, ROWS)], m.at[plane, me, pl.ds(0, ROWS)], own_sem.at[plane]
        )
        for plane in range(PLANES)
    ]
    for copy in own:
        copy.start()
    for j in range(GROUPS):
        lamb[me, j : j + 1, :] = jnp.full((1, NZ), eig[j], jnp.float32)
    pl.semaphore_wait(barrier, GROUPS - 1 + SECTORS - 1)

    def piece_copy(index, dest, origin):
        plane, row, rows = PIECES[index]
        return pltpu.make_async_remote_copy(
            src_ref=src.at[plane, pl.ds(first_row(dest) + row, rows)],
            dst_ref=m.at[plane, origin, pl.ds(row, rows)],
            send_sem=send_sem.at[index, dest],
            recv_sem=recv_sem.at[index, origin],
            device_id=(sec, dest),
            device_id_type=MESH,
        )

    def lam_copy(dest, origin):
        return pltpu.make_async_remote_copy(
            src_ref=lamb.at[me],
            dst_ref=lamb.at[origin],
            send_sem=lam_send.at[dest],
            recv_sem=lam_recv.at[origin],
            device_id=(sec, dest),
            device_id_type=MESH,
        )

    thick_copy = pltpu.make_async_remote_copy(
        src_ref=thick.at[0],
        dst_ref=thk,
        send_sem=thick_sem.at[0],
        recv_sem=thick_sem.at[1],
        device_id=(before, me),
        device_id_type=MESH,
    )
    thick_copy.start()
    def send(index):
        @pl.loop(1, GROUPS)
        def _(off):
            piece_copy(index, peer(off), me).start()

    send(0)

    @pl.loop(1, GROUPS)
    def _(off):
        lam_copy(peer(off), me).start()

    for index in range(1, len(PIECES)):
        send(index)

    acc[...] = jnp.zeros_like(acc)
    line = lax.broadcasted_iota(jnp.int32, (16, NZ), 0)
    diff = line - lax.broadcasted_iota(jnp.int32, (16, NZ), 1)
    for e in range(3):
        bands[e] = jnp.where(lax.rem(diff + 1 - e + 128, 16) == 0, 1.0, 0.0).astype(jnp.bfloat16)
    for i in range(8):
        bands[3 + i] = jnp.where(jnp.abs(diff + 16 * i) <= 1, 1.0, 0.0).astype(jnp.bfloat16)
    trow[...] = jnp.zeros_like(trow)

    def thick_rows(plane, ref):
        @pl.loop(0, ROWS)
        def _(l):
            y = lax.rem(own_first + l, NY)
            trow[1, plane, pl.ds(8 + l, 1), :] = ref[pl.ds(y, 1), :]

        trow[0, plane] = pltpu.roll(trow[1, plane], 1, axis=1)
        trow[2, plane] = pltpu.roll(trow[1, plane], NZ - 1, axis=1)

    def coefficients(u, plane, plane_out):
        centre = trow[1, plane_out, pl.ds(8, ROWS), :]
        for b in range(3):
            for e in range(3):
                both = 0.5 * (centre + trow[e, plane, pl.ds(7 + b, ROWS), :])
                k = 9 * (plane - plane_out + 1) + 3 * b + e
                for half, table in enumerate((stiff, mass)):
                    coeffs[u, b, half, e] = both * table[k]

    def banded(u, l, put):
        on = [bands[e] > 0 for e in range(2)]
        tiles = {}
        for b in range(3):
            for half in range(2):
                lines = [
                    jnp.broadcast_to(coeffs[u, b, half, e, pl.ds(l, 1), :], (16, NZ)).astype(
                        jnp.bfloat16
                    )
                    for e in range(3)
                ]
                tiles[b, half] = jnp.where(
                    on[0], lines[0], jnp.where(on[1], lines[1], lines[2])
                )
        zero = jnp.zeros((16, NZ), jnp.bfloat16)
        for i in range(8):
            keep = bands[3 + i] > 0
            for (b, half), tile in tiles.items():
                first = b * NZ + 16 * i
                put(
                    slice(first, first + 16),
                    slice(half * NZ, (half + 1) * NZ),
                    jnp.where(keep, tile, zero),
                )

    def matrices(buf, pairs):
        for u, (plane, plane_out) in enumerate(pairs):
            coefficients(u, plane, plane_out)

        @pl.loop(0, ROWS)
        def _(l):

            @pl.loop(0, len(pairs))
            def _(u):
                def put(rows, columns, tile):
                    matrix[buf, u, l, rows, columns] = tile

                banded(u, l, put)

    for plane in range(PLANES):
        thick_rows(plane, thick.at[plane])
    thick_copy.wait()
    thick_rows(PLANES, thk)

    last_group = me == GROUPS - 1
    end_sector = sec == SECTORS - 1

    def source_row(l, b, cross_end):
        if b == 0:
            ok = jnp.where(last_group, l >= 1, l < ROWS - 1)
        else:
            low = l if b == 1 else l - 1
            ok = jnp.where(last_group, low >= 1, low >= 0) & (low < ROWS - 1)
            ok = ok & (lax.rem(own_first + low + 1, NY) != 0)
        if cross_end:
            ok = ok & jnp.logical_not(end_sector)
        return jnp.where(ok, l + b, ROWS)

    def image_of(l, plane, plane_out, held):
        fields = []
        for b in (-1, 0, 1):
            r = source_row(l, b, max(plane, plane_out) == PLANES)
            fields.append(m[plane, :, r].reshape(MODES, NZ))
        return jnp.dot(
            jnp.concatenate(fields, axis=1),
            held[...],
            preferred_element_type=jnp.float32,
        )

    def row_step(l, plane, outs):
        loads, rows = [], []
        for plane_out, buf, u, begun, complete in outs:
            image = image_of(l, plane, plane_out, matrix.at[buf, u, l])
            slot = plane_out % 3
            if not begun:
                image = image + images[slot, l]
            if not complete:
                images[slot, l] = image
                continue
            lam = lamb[...].reshape(MODES, NZ)
            load = image[:, :NZ] - lam * image[:, NZ:]
            high = load.astype(jnp.bfloat16)
            loads += [high, (load - high.astype(jnp.float32)).astype(jnp.bfloat16)]
            rows += [m[plane_out, :, l].reshape(MODES, NZ)] * 2
        if loads:
            gram = lax.dot_general(
                jnp.concatenate(loads, axis=1),
                jnp.concatenate(rows, axis=1),
                (((1,), (1,)), ((), ())),
                preferred_element_type=jnp.float32,
            )
            acc[...] += gram.reshape(GROUPS, 16, MODES)

    def process(plane, outs, low, high):
        @pl.loop(low, high)
        def _(l):
            row_step(l, plane, outs)

    def arrived(index):
        @pl.loop(1, GROUPS)
        def _(off):
            piece_copy(index, me, peer(off)).wait_recv()

    matrices(0, ((0, 0), (0, 1)))
    matrices(1, ((1, 0), (1, 1), (1, 2)))
    arrived(0)
    own[0].wait()
    rim = pltpu.make_async_remote_copy(
        src_ref=m.at[0],
        dst_ref=m.at[PLANES],
        send_sem=rim_sem.at[0],
        recv_sem=rim_sem.at[1],
        device_id=(before, me),
        device_id_type=MESH,
    )
    rim.start()

    @pl.loop(1, GROUPS)
    def _(off):
        lam_copy(me, peer(off)).wait_recv()

    process(0, [(0, 0, 0, True, False), (1, 0, 1, True, False)], 0, ROWS)
    matrices(0, ((2, 1), (2, 2), (2, 3)))
    arrived(1)
    own[1].wait()
    process(
        1, [(0, 1, 0, False, True), (1, 1, 1, False, False), (2, 1, 2, True, False)], 0, ROWS
    )
    matrices(1, ((3, 2), (3, 3), (3, 4)))
    rim.wait()
    coefficients(0, PLANES, PLANES - 1)

    @pl.loop(0, ROWS)
    def _(l):
        def put(rows, columns, tile):
            single[rows, columns] = tile

        banded(0, l, put)
        images[(PLANES - 1) % 3, l] = image_of(l, PLANES, PLANES - 1, single)

    arrived(2)
    own[2].wait()
    process(
        2, [(1, 0, 0, False, True), (2, 0, 1, False, False), (3, 0, 2, False, False)], 0, ROWS
    )
    own[3].wait()
    for index, low, high in ((3, 0, 7), (4, 7, 11), (5, 11, ROWS)):
        arrived(index)
        process(
            3,
            [(2, 1, 0, False, True), (3, 1, 1, False, True), (4, 1, 2, True, True)],
            low,
            high,
        )

    def sum_copy(dest, origin):
        return pltpu.make_async_remote_copy(
            src_ref=acc.at[dest],
            dst_ref=sums.at[origin],
            send_sem=sum_send.at[dest],
            recv_sem=sum_recv.at[origin],
            device_id=(sec, dest),
            device_id_type=MESH,
        )

    @pl.loop(1, GROUPS)
    def _(off):
        sum_copy(peer(off), me).start()

    sums[me] = acc[me]

    @pl.loop(1, GROUPS)
    def _(off):
        sum_copy(me, peer(off)).wait_recv()

    total = sums[0]
    for p in range(1, GROUPS):
        total = total + sums[p]
    for s in range(SECTORS):
        parts[s, :, 0:32] = total[:, 32 * s : 32 * s + 32]
        parts[s, :, 32:NZ] = jnp.zeros((16, NZ - 32), jnp.float32)

    def block_copy(dest, origin):
        return pltpu.make_async_remote_copy(
            src_ref=parts.at[dest],
            dst_ref=blocks.at[origin],
            send_sem=blk_send.at[dest],
            recv_sem=blk_recv.at[origin],
            device_id=(dest, me),
            device_id_type=MESH,
        )

    @pl.loop(1, SECTORS)
    def _(off):
        block_copy(lax.rem(sec + off, SECTORS), sec).start()

    blocks[sec] = parts[sec]

    @pl.loop(1, SECTORS)
    def _(off):
        block_copy(sec, lax.rem(sec + off, SECTORS)).wait_recv()

    block = blocks[0]
    for s in range(1, SECTORS):
        block = block + blocks[s]
    out[...] = jnp.transpose(block)[0:32, :]

    for index in range(len(PIECES)):

        @pl.loop(1, GROUPS)
        def _(off, index=index):
            piece_copy(index, peer(off), me).wait_send()

    @pl.loop(1, GROUPS)
    def _(off):
        lam_copy(peer(off), me).wait_send()
        sum_copy(peer(off), me).wait_send()

    @pl.loop(1, SECTORS)
    def _(off):
        block_copy(lax.rem(sec + off, SECTORS), sec).wait_send()


def on_device(modes, thickness, stiff_taps, mass_taps, eigenvalues):
    src = modes.transpose(2, 1, 3, 0, 4).reshape(PLANES, ALL_ROWS, 16, NZ)
    smem = pl.BlockSpec(memory_space=pltpu.SMEM)
    vmem = pl.BlockSpec(memory_space=pltpu.VMEM)
    dma = pltpu.SemaphoreType.DMA
    f32 = jnp.float32
    return pl.pallas_call(
        kernel,
        out_shape=jax.ShapeDtypeStruct((32, 16), f32),
        in_specs=[pl.BlockSpec(memory_space=pl.ANY), vmem, smem, smem, smem],
        out_specs=vmem,
        scratch_shapes=[
            pltpu.VMEM((PLANES + 1, GROUPS, ROWS + 1, 16, NZ), jnp.bfloat16),
            pltpu.VMEM((3, ROWS, MODES, 2 * NZ), f32),
            pltpu.VMEM((2, 3, ROWS, 3 * NZ, 2 * NZ), jnp.bfloat16),
            pltpu.VMEM((3 * NZ, 2 * NZ), jnp.bfloat16),
            pltpu.VMEM((3, 3, 2, 3, ROWS, NZ), f32),
            pltpu.VMEM((11, 16, NZ), jnp.bfloat16),
            pltpu.VMEM((NY, NZ), f32),
            pltpu.VMEM((3, PLANES + 1, 32, NZ), f32),
            pltpu.VMEM((GROUPS, 16, NZ), f32),
            pltpu.VMEM((GROUPS, 16, MODES), f32),
            pltpu.VMEM((GROUPS, 16, MODES), f32),
            pltpu.VMEM((SECTORS, 16, NZ), f32),
            pltpu.VMEM((SECTORS, 16, NZ), f32),
            dma((len(PIECES), GROUPS)),
            dma((len(PIECES), GROUPS)),
            dma((PLANES,)),
            dma((2,)),
            dma((2,)),
            dma((GROUPS,)),
            dma((GROUPS,)),
            dma((GROUPS,)),
            dma((GROUPS,)),
            dma((SECTORS,)),
            dma((SECTORS,)),
        ],
        compiler_params=pltpu.CompilerParams(
            collective_id=0, has_side_effects=True, vmem_limit_bytes=42 * 2**20
        ),
    )(src, thickness, stiff_taps, mass_taps, eigenvalues)


def solution(mesh):
    in_specs = (P("mode", None, "sector", None, None), P("sector", None, None), P(), P(), P("mode"))
    return jax.shard_map(
        on_device, mesh=mesh, in_specs=in_specs, out_specs=P("sector", "mode"), check_vma=False
    )
```

```python
import functools

import jax
import jax.numpy as jnp
from jax import lax
from jax.experimental import pallas as pl
from jax.experimental.pallas import tpu as pltpu
from jax.sharding import PartitionSpec as P

MESH = pl.DeviceIdType.MESH
GROUPS = 16
SECTORS = 8
OWN = 15
ROWS = 16
PLANES = 4
NZ = 128
MODES = 256
NY = 80
STEP = 4
ALL_ROWS = 240
PIECES = ((0, 0, 16), (1, 0, 16), (2, 0, 16), (3, 0, 16))


def kernel(
    src, thick, stiff, mass, eig, out,
    m, images, matrix, single, coeffs, bands, thk, trow, lamb, acc, sums, parts, blocks,
    send_sem, recv_sem, own_sem, rim_sem, thick_sem, lam_send, lam_recv, sum_send, sum_recv, blk_send, blk_recv,
):
    sec = lax.axis_index("sector")
    me = lax.axis_index("mode")
    me_x = lax.rem(me, 4)
    me_y = lax.div(me, 4)
    before = lax.rem(sec + SECTORS - 1, SECTORS)

    def peer(off):
        dx = lax.rem(off, 4)
        dy = lax.div(off, 4)
        return lax.rem(me_y + dy, 4) * 4 + lax.rem(me_x + dx, 4)

    def first_row(group):
        return jnp.minimum(group * OWN, ALL_ROWS - ROWS)

    m[:, :, ROWS] = jnp.zeros((PLANES + 1, GROUPS, 16, NZ), jnp.bfloat16)
    barrier = pltpu.get_barrier_semaphore()

    @pl.loop(1, GROUPS)
    def _(off):
        pl.semaphore_signal(barrier, inc=1, device_id=(sec, peer(off)), device_id_type=MESH)

    @pl.loop(1, SECTORS)
    def _(off):
        pl.semaphore_signal(
            barrier, inc=1, device_id=(lax.rem(sec + off, SECTORS), me), device_id_type=MESH
        )

    own_first = first_row(me)
    own = [
        pltpu.make_async_copy(
            src.at[plane, pl.ds(own_first, ROWS)], m.at[plane, me, pl.ds(0, ROWS)], own_sem.at[plane]
        )
        for plane in range(PLANES)
    ]
    for copy in own:
        copy.start()
    for j in range(GROUPS):
        lamb[me, j : j + 1, :] = jnp.full((1, NZ), eig[j], jnp.float32)
    pl.semaphore_wait(barrier, GROUPS - 1 + SECTORS - 1)

    def piece_copy(index, dest, origin):
        plane, row, rows = PIECES[index]
        return pltpu.make_async_remote_copy(
            src_ref=src.at[plane, pl.ds(first_row(dest) + row, rows)],
            dst_ref=m.at[plane, origin, pl.ds(row, rows)],
            send_sem=send_sem.at[index, dest],
            recv_sem=recv_sem.at[index, origin],
            device_id=(sec, dest),
            device_id_type=MESH,
        )

    def lam_copy(dest, origin):
        return pltpu.make_async_remote_copy(
            src_ref=lamb.at[me],
            dst_ref=lamb.at[origin],
            send_sem=lam_send.at[dest],
            recv_sem=lam_recv.at[origin],
            device_id=(sec, dest),
            device_id_type=MESH,
        )

    thick_copy = pltpu.make_async_remote_copy(
        src_ref=thick.at[0],
        dst_ref=thk,
        send_sem=thick_sem.at[0],
        recv_sem=thick_sem.at[1],
        device_id=(before, me),
        device_id_type=MESH,
    )
    thick_copy.start()
    def send(index):
        @pl.loop(1, GROUPS)
        def _(off):
            piece_copy(index, peer(off), me).start()

    send(0)

    @pl.loop(1, GROUPS)
    def _(off):
        lam_copy(peer(off), me).start()

    for index in range(1, len(PIECES)):
        send(index)

    acc[...] = jnp.zeros_like(acc)
    line = lax.broadcasted_iota(jnp.int32, (16, NZ), 0)
    diff = line - lax.broadcasted_iota(jnp.int32, (16, NZ), 1)
    for e in range(3):
        bands[e] = jnp.where(lax.rem(diff + 1 - e + 128, 16) == 0, 1.0, 0.0).astype(jnp.bfloat16)
    for i in range(8):
        bands[3 + i] = jnp.where(jnp.abs(diff + 16 * i) <= 1, 1.0, 0.0).astype(jnp.bfloat16)
    trow[...] = jnp.zeros_like(trow)

    def thick_rows(plane, ref):
        @pl.loop(0, ROWS)
        def _(l):
            y = lax.rem(own_first + l, NY)
            trow[1, plane, pl.ds(8 + l, 1), :] = ref[pl.ds(y, 1), :]

        trow[0, plane] = pltpu.roll(trow[1, plane], 1, axis=1)
        trow[2, plane] = pltpu.roll(trow[1, plane], NZ - 1, axis=1)

    def coefficients(u, plane, plane_out):
        centre = trow[1, plane_out, pl.ds(8, ROWS), :]
        for b in range(3):
            for e in range(3):
                both = 0.5 * (centre + trow[e, plane, pl.ds(7 + b, ROWS), :])
                k = 9 * (plane - plane_out + 1) + 3 * b + e
                for half, table in enumerate((stiff, mass)):
                    coeffs[u, b, half, e] = both * table[k]

    def banded(u, l, put):
        on = [bands[e] > 0 for e in range(2)]
        tiles = {}
        for b in range(3):
            for half in range(2):
                lines = [
                    jnp.broadcast_to(coeffs[u, b, half, e, pl.ds(l, 1), :], (16, NZ)).astype(
                        jnp.bfloat16
                    )
                    for e in range(3)
                ]
                tiles[b, half] = jnp.where(
                    on[0], lines[0], jnp.where(on[1], lines[1], lines[2])
                )
        zero = jnp.zeros((16, NZ), jnp.bfloat16)
        for i in range(8):
            keep = bands[3 + i] > 0
            for (b, half), tile in tiles.items():
                first = b * NZ + 16 * i
                put(
                    slice(first, first + 16),
                    slice(half * NZ, (half + 1) * NZ),
                    jnp.where(keep, tile, zero),
                )

    def matrices(buf, pairs):
        for u, (plane, plane_out) in enumerate(pairs):
            coefficients(u, plane, plane_out)

        @pl.loop(0, ROWS)
        def _(l):

            @pl.loop(0, len(pairs))
            def _(u):
                def put(rows, columns, tile):
                    matrix[buf, u, l, rows, columns] = tile

                banded(u, l, put)

    for plane in range(PLANES):
        thick_rows(plane, thick.at[plane])
    thick_copy.wait()
    thick_rows(PLANES, thk)

    last_group = me == GROUPS - 1
    end_sector = sec == SECTORS - 1

    def source_row(l, b, cross_end):
        if b == 0:
            ok = jnp.where(last_group, l >= 1, l < ROWS - 1)
        else:
            low = l if b == 1 else l - 1
            ok = jnp.where(last_group, low >= 1, low >= 0) & (low < ROWS - 1)
            ok = ok & (lax.rem(own_first + low + 1, NY) != 0)
        if cross_end:
            ok = ok & jnp.logical_not(end_sector)
        return jnp.where(ok, l + b, ROWS)

    def image_of(l, plane, plane_out, held):
        fields = []
        for b in (-1, 0, 1):
            r = source_row(l, b, max(plane, plane_out) == PLANES)
            fields.append(m[plane, :, r].reshape(MODES, NZ))
        return jnp.dot(
            jnp.concatenate(fields, axis=1),
            held[...],
            preferred_element_type=jnp.float32,
        )

    def row_step(l, plane, outs, loads, rows):
        for plane_out, buf, u, begun, complete in outs:
            image = image_of(l, plane, plane_out, matrix.at[buf, u, l])
            slot = plane_out % 3
            if not begun:
                image = image + images[slot, l]
            if not complete:
                images[slot, l] = image
                continue
            lam = lamb[...].reshape(MODES, NZ)
            load = image[:, :NZ] - lam * image[:, NZ:]
            high = load.astype(jnp.bfloat16)
            loads += [high, (load - high.astype(jnp.float32)).astype(jnp.bfloat16)]
            rows += [m[plane_out, :, l].reshape(MODES, NZ)] * 2

    def process(plane, outs, low, high):
        @pl.loop(0, (high - low) // STEP)
        def _(pair):
            loads, rows = [], []
            for other in range(STEP):
                row_step(low + STEP * pair + other, plane, outs, loads, rows)
            if loads:
                gram = lax.dot_general(
                    jnp.concatenate(loads, axis=1),
                    jnp.concatenate(rows, axis=1),
                    (((1,), (1,)), ((), ())),
                    preferred_element_type=jnp.float32,
                )
                acc[...] += gram.reshape(GROUPS, 16, MODES)

    def arrived(index):
        @pl.loop(1, GROUPS)
        def _(off):
            piece_copy(index, me, peer(off)).wait_recv()

    matrices(0, ((0, 0), (0, 1)))
    matrices(1, ((1, 0), (1, 1), (1, 2)))
    arrived(0)
    own[0].wait()
    rim = pltpu.make_async_remote_copy(
        src_ref=m.at[0],
        dst_ref=m.at[PLANES],
        send_sem=rim_sem.at[0],
        recv_sem=rim_sem.at[1],
        device_id=(before, me),
        device_id_type=MESH,
    )
    rim.start()

    @pl.loop(1, GROUPS)
    def _(off):
        lam_copy(me, peer(off)).wait_recv()

    process(0, [(0, 0, 0, True, False), (1, 0, 1, True, False)], 0, ROWS)
    matrices(0, ((2, 1), (2, 2), (2, 3)))
    arrived(1)
    own[1].wait()
    process(
        1, [(0, 1, 0, False, True), (1, 1, 1, False, False), (2, 1, 2, True, False)], 0, ROWS
    )
    matrices(1, ((3, 2), (3, 3), (3, 4)))
    rim.wait()
    coefficients(0, PLANES, PLANES - 1)

    @pl.loop(0, ROWS)
    def _(l):
        def put(rows, columns, tile):
            single[rows, columns] = tile

        banded(0, l, put)
        images[(PLANES - 1) % 3, l] = image_of(l, PLANES, PLANES - 1, single)

    arrived(2)
    own[2].wait()
    process(
        2, [(1, 0, 0, False, True), (2, 0, 1, False, False), (3, 0, 2, False, False)], 0, ROWS
    )
    own[3].wait()
    for index, low, high in ((3, 0, ROWS),):
        arrived(index)
        process(
            3,
            [(2, 1, 0, False, True), (3, 1, 1, False, True), (4, 1, 2, True, True)],
            low,
            high,
        )

    def sum_copy(dest, origin):
        return pltpu.make_async_remote_copy(
            src_ref=acc.at[dest],
            dst_ref=sums.at[origin],
            send_sem=sum_send.at[dest],
            recv_sem=sum_recv.at[origin],
            device_id=(sec, dest),
            device_id_type=MESH,
        )

    @pl.loop(1, GROUPS)
    def _(off):
        sum_copy(peer(off), me).start()

    sums[me] = acc[me]

    @pl.loop(1, GROUPS)
    def _(off):
        sum_copy(me, peer(off)).wait_recv()

    total = sums[0]
    for p in range(1, GROUPS):
        total = total + sums[p]
    for s in range(SECTORS):
        parts[s, :, 0:32] = total[:, 32 * s : 32 * s + 32]
        parts[s, :, 32:NZ] = jnp.zeros((16, NZ - 32), jnp.float32)

    def block_copy(dest, origin):
        return pltpu.make_async_remote_copy(
            src_ref=parts.at[dest],
            dst_ref=blocks.at[origin],
            send_sem=blk_send.at[dest],
            recv_sem=blk_recv.at[origin],
            device_id=(dest, me),
            device_id_type=MESH,
        )

    @pl.loop(1, SECTORS)
    def _(off):
        block_copy(lax.rem(sec + off, SECTORS), sec).start()

    blocks[sec] = parts[sec]

    @pl.loop(1, SECTORS)
    def _(off):
        block_copy(sec, lax.rem(sec + off, SECTORS)).wait_recv()

    block = blocks[0]
    for s in range(1, SECTORS):
        block = block + blocks[s]
    out[...] = jnp.transpose(block)[0:32, :]

    for index in range(len(PIECES)):

        @pl.loop(1, GROUPS)
        def _(off, index=index):
            piece_copy(index, peer(off), me).wait_send()

    @pl.loop(1, GROUPS)
    def _(off):
        lam_copy(peer(off), me).wait_send()
        sum_copy(peer(off), me).wait_send()

    @pl.loop(1, SECTORS)
    def _(off):
        block_copy(lax.rem(sec + off, SECTORS), sec).wait_send()


def on_device(modes, thickness, stiff_taps, mass_taps, eigenvalues):
    src = modes.transpose(2, 1, 3, 0, 4).reshape(PLANES, ALL_ROWS, 16, NZ)
    smem = pl.BlockSpec(memory_space=pltpu.SMEM)
    vmem = pl.BlockSpec(memory_space=pltpu.VMEM)
    dma = pltpu.SemaphoreType.DMA
    f32 = jnp.float32
    return pl.pallas_call(
        kernel,
        out_shape=jax.ShapeDtypeStruct((32, 16), f32),
        in_specs=[pl.BlockSpec(memory_space=pl.ANY), vmem, smem, smem, smem],
        out_specs=vmem,
        scratch_shapes=[
            pltpu.VMEM((PLANES + 1, GROUPS, ROWS + 1, 16, NZ), jnp.bfloat16),
            pltpu.VMEM((3, ROWS, MODES, 2 * NZ), f32),
            pltpu.VMEM((2, 3, ROWS, 3 * NZ, 2 * NZ), jnp.bfloat16),
            pltpu.VMEM((3 * NZ, 2 * NZ), jnp.bfloat16),
            pltpu.VMEM((3, 3, 2, 3, ROWS, NZ), f32),
            pltpu.VMEM((11, 16, NZ), jnp.bfloat16),
            pltpu.VMEM((NY, NZ), f32),
            pltpu.VMEM((3, PLANES + 1, 32, NZ), f32),
            pltpu.VMEM((GROUPS, 16, NZ), f32),
            pltpu.VMEM((GROUPS, 16, MODES), f32),
            pltpu.VMEM((GROUPS, 16, MODES), f32),
            pltpu.VMEM((SECTORS, 16, NZ), f32),
            pltpu.VMEM((SECTORS, 16, NZ), f32),
            dma((len(PIECES), GROUPS)),
            dma((len(PIECES), GROUPS)),
            dma((PLANES,)),
            dma((2,)),
            dma((2,)),
            dma((GROUPS,)),
            dma((GROUPS,)),
            dma((GROUPS,)),
            dma((GROUPS,)),
            dma((SECTORS,)),
            dma((SECTORS,)),
        ],
        compiler_params=pltpu.CompilerParams(
            collective_id=0, has_side_effects=True, vmem_limit_bytes=42 * 2**20
        ),
    )(src, thickness, stiff_taps, mass_taps, eigenvalues)


def solution(mesh):
    in_specs = (P("mode", None, "sector", None, None), P("sector", None, None), P(), P(), P("mode"))
    return jax.shard_map(
        on_device, mesh=mesh, in_specs=in_specs, out_specs=P("sector", "mode"), check_vma=False
    )
```

```python
import functools

import jax
import jax.numpy as jnp
from jax import lax
from jax.experimental import pallas as pl
from jax.experimental.pallas import tpu as pltpu
from jax.sharding import PartitionSpec as P

MESH = pl.DeviceIdType.MESH
GROUPS = 16
SECTORS = 8
OWN = 15
ROWS = 16
PLANES = 4
NZ = 128
MODES = 256
NY = 80
STEP = 4
ALL_ROWS = 240
PIECES = ((0, 0, 16), (1, 0, 16), (2, 0, 16), (3, 0, 9), (3, 9, 7))


def kernel(
    src, thick, stiff, mass, eig, out,
    m, images, matrix, single, coeffs, bands, thk, trow, lamb, acc, sums, parts, blocks,
    send_sem, recv_sem, own_sem, rim_sem, thick_sem, lam_send, lam_recv, sum_send, sum_recv, blk_send, blk_recv,
):
    sec = lax.axis_index("sector")
    me = lax.axis_index("mode")
    me_x = lax.rem(me, 4)
    me_y = lax.div(me, 4)
    before = lax.rem(sec + SECTORS - 1, SECTORS)

    def peer(off):
        dx = lax.rem(off, 4)
        dy = lax.div(off, 4)
        return lax.rem(me_y + dy, 4) * 4 + lax.rem(me_x + dx, 4)

    def first_row(group):
        return jnp.minimum(group * OWN, ALL_ROWS - ROWS)

    m[:, :, ROWS] = jnp.zeros((PLANES + 1, GROUPS, 16, NZ), jnp.bfloat16)
    barrier = pltpu.get_barrier_semaphore()

    @pl.loop(1, GROUPS)
    def _(off):
        pl.semaphore_signal(barrier, inc=1, device_id=(sec, peer(off)), device_id_type=MESH)

    @pl.loop(1, SECTORS)
    def _(off):
        pl.semaphore_signal(
            barrier, inc=1, device_id=(lax.rem(sec + off, SECTORS), me), device_id_type=MESH
        )

    own_first = first_row(me)
    own = [
        pltpu.make_async_copy(
            src.at[plane, pl.ds(own_first, ROWS)], m.at[plane, me, pl.ds(0, ROWS)], own_sem.at[plane]
        )
        for plane in range(PLANES)
    ]
    for copy in own:
        copy.start()
    for j in range(GROUPS):
        lamb[me, j : j + 1, :] = jnp.full((1, NZ), eig[j], jnp.float32)
    pl.semaphore_wait(barrier, GROUPS - 1 + SECTORS - 1)

    def piece_copy(index, dest, origin):
        plane, row, rows = PIECES[index]
        return pltpu.make_async_remote_copy(
            src_ref=src.at[plane, pl.ds(first_row(dest) + row, rows)],
            dst_ref=m.at[plane, origin, pl.ds(row, rows)],
            send_sem=send_sem.at[index, dest],
            recv_sem=recv_sem.at[index, origin],
            device_id=(sec, dest),
            device_id_type=MESH,
        )

    def lam_copy(dest, origin):
        return pltpu.make_async_remote_copy(
            src_ref=lamb.at[me],
            dst_ref=lamb.at[origin],
            send_sem=lam_send.at[dest],
            recv_sem=lam_recv.at[origin],
            device_id=(sec, dest),
            device_id_type=MESH,
        )

    thick_copy = pltpu.make_async_remote_copy(
        src_ref=thick.at[0],
        dst_ref=thk,
        send_sem=thick_sem.at[0],
        recv_sem=thick_sem.at[1],
        device_id=(before, me),
        device_id_type=MESH,
    )
    thick_copy.start()
    def send(index):
        @pl.loop(1, GROUPS)
        def _(off):
            piece_copy(index, peer(off), me).start()

    send(0)

    @pl.loop(1, GROUPS)
    def _(off):
        lam_copy(peer(off), me).start()

    for index in range(1, len(PIECES)):
        send(index)

    acc[...] = jnp.zeros_like(acc)
    line = lax.broadcasted_iota(jnp.int32, (16, NZ), 0)
    diff = line - lax.broadcasted_iota(jnp.int32, (16, NZ), 1)
    for e in range(3):
        bands[e] = jnp.where(lax.rem(diff + 1 - e + 128, 16) == 0, 1.0, 0.0).astype(jnp.bfloat16)
    for i in range(8):
        bands[3 + i] = jnp.where(jnp.abs(diff + 16 * i) <= 1, 1.0, 0.0).astype(jnp.bfloat16)
    trow[...] = jnp.zeros_like(trow)

    def thick_rows(plane, ref):
        @pl.loop(0, ROWS)
        def _(l):
            y = lax.rem(own_first + l, NY)
            trow[1, plane, pl.ds(8 + l, 1), :] = ref[pl.ds(y, 1), :]

        trow[0, plane] = pltpu.roll(trow[1, plane], 1, axis=1)
        trow[2, plane] = pltpu.roll(trow[1, plane], NZ - 1, axis=1)

    def coefficients(u, plane, plane_out):
        centre = trow[1, plane_out, pl.ds(8, ROWS), :]
        for b in range(3):
            for e in range(3):
                both = 0.5 * (centre + trow[e, plane, pl.ds(7 + b, ROWS), :])
                k = 9 * (plane - plane_out + 1) + 3 * b + e
                for half, table in enumerate((stiff, mass)):
                    coeffs[u, b, half, e] = both * table[k]

    def banded(u, l, put):
        on = [bands[e] > 0 for e in range(2)]
        tiles = {}
        for b in range(3):
            for half in range(2):
                lines = [
                    jnp.broadcast_to(coeffs[u, b, half, e, pl.ds(l, 1), :], (16, NZ)).astype(
                        jnp.bfloat16
                    )
                    for e in range(3)
                ]
                tiles[b, half] = jnp.where(
                    on[0], lines[0], jnp.where(on[1], lines[1], lines[2])
                )
        zero = jnp.zeros((16, NZ), jnp.bfloat16)
        for i in range(8):
            keep = bands[3 + i] > 0
            for (b, half), tile in tiles.items():
                first = b * NZ + 16 * i
                put(
                    slice(first, first + 16),
                    slice(half * NZ, (half + 1) * NZ),
                    jnp.where(keep, tile, zero),
                )

    def matrices(buf, pairs):
        for u, (plane, plane_out) in enumerate(pairs):
            coefficients(u, plane, plane_out)

        @pl.loop(0, ROWS)
        def _(l):

            @pl.loop(0, len(pairs))
            def _(u):
                def put(rows, columns, tile):
                    matrix[buf, u, l, rows, columns] = tile

                banded(u, l, put)

    for plane in range(PLANES):
        thick_rows(plane, thick.at[plane])
    thick_copy.wait()
    thick_rows(PLANES, thk)

    last_group = me == GROUPS - 1
    end_sector = sec == SECTORS - 1

    def source_row(l, b, cross_end):
        if b == 0:
            ok = jnp.where(last_group, l >= 1, l < ROWS - 1)
        else:
            low = l if b == 1 else l - 1
            ok = jnp.where(last_group, low >= 1, low >= 0) & (low < ROWS - 1)
            ok = ok & (lax.rem(own_first + low + 1, NY) != 0)
        if cross_end:
            ok = ok & jnp.logical_not(end_sector)
        return jnp.where(ok, l + b, ROWS)

    def image_of(l, plane, plane_out, held):
        fields = []
        for b in (-1, 0, 1):
            r = source_row(l, b, max(plane, plane_out) == PLANES)
            fields.append(m[plane, :, r].reshape(MODES, NZ))
        return jnp.dot(
            jnp.concatenate(fields, axis=1),
            held[...],
            preferred_element_type=jnp.float32,
        )

    def row_step(l, plane, outs, loads, rows):
        for plane_out, buf, u, begun, complete in outs:
            image = image_of(l, plane, plane_out, matrix.at[buf, u, l])
            slot = plane_out % 3
            if not begun:
                image = image + images[slot, l]
            if not complete:
                images[slot, l] = image
                continue
            lam = lamb[...].reshape(MODES, NZ)
            load = image[:, :NZ] - lam * image[:, NZ:]
            high = load.astype(jnp.bfloat16)
            loads += [high, (load - high.astype(jnp.float32)).astype(jnp.bfloat16)]
            rows += [m[plane_out, :, l].reshape(MODES, NZ)] * 2

    def process(plane, outs, low, high):
        @pl.loop(0, (high - low) // STEP)
        def _(pair):
            loads, rows = [], []
            for other in range(STEP):
                row_step(low + STEP * pair + other, plane, outs, loads, rows)
            if loads:
                gram = lax.dot_general(
                    jnp.concatenate(loads, axis=1),
                    jnp.concatenate(rows, axis=1),
                    (((1,), (1,)), ((), ())),
                    preferred_element_type=jnp.float32,
                )
                acc[...] += gram.reshape(GROUPS, 16, MODES)

    def arrived(index):
        @pl.loop(1, GROUPS)
        def _(off):
            piece_copy(index, me, peer(off)).wait_recv()

    matrices(0, ((0, 0), (0, 1)))
    matrices(1, ((1, 0), (1, 1), (1, 2)))
    arrived(0)
    own[0].wait()
    rim = pltpu.make_async_remote_copy(
        src_ref=m.at[0],
        dst_ref=m.at[PLANES],
        send_sem=rim_sem.at[0],
        recv_sem=rim_sem.at[1],
        device_id=(before, me),
        device_id_type=MESH,
    )
    rim.start()

    @pl.loop(1, GROUPS)
    def _(off):
        lam_copy(me, peer(off)).wait_recv()

    process(0, [(0, 0, 0, True, False), (1, 0, 1, True, False)], 0, ROWS)
    matrices(0, ((2, 1), (2, 2), (2, 3)))
    arrived(1)
    own[1].wait()
    process(
        1, [(0, 1, 0, False, True), (1, 1, 1, False, False), (2, 1, 2, True, False)], 0, ROWS
    )
    matrices(1, ((3, 2), (3, 3), (3, 4)))
    rim.wait()
    coefficients(0, PLANES, PLANES - 1)

    @pl.loop(0, ROWS)
    def _(l):
        def put(rows, columns, tile):
            single[rows, columns] = tile

        banded(0, l, put)
        images[(PLANES - 1) % 3, l] = image_of(l, PLANES, PLANES - 1, single)

    arrived(2)
    own[2].wait()
    process(
        2, [(1, 0, 0, False, True), (2, 0, 1, False, False), (3, 0, 2, False, False)], 0, ROWS
    )
    own[3].wait()
    for index, low, high in ((3, 0, 8), (4, 8, ROWS)):
        arrived(index)
        process(
            3,
            [(2, 1, 0, False, True), (3, 1, 1, False, True), (4, 1, 2, True, True)],
            low,
            high,
        )

    def sum_copy(dest, origin):
        return pltpu.make_async_remote_copy(
            src_ref=acc.at[dest],
            dst_ref=sums.at[origin],
            send_sem=sum_send.at[dest],
            recv_sem=sum_recv.at[origin],
            device_id=(sec, dest),
            device_id_type=MESH,
        )

    @pl.loop(1, GROUPS)
    def _(off):
        sum_copy(peer(off), me).start()

    sums[me] = acc[me]

    @pl.loop(1, GROUPS)
    def _(off):
        sum_copy(me, peer(off)).wait_recv()

    total = sums[0]
    for p in range(1, GROUPS):
        total = total + sums[p]
    for s in range(SECTORS):
        parts[s, :, 0:32] = total[:, 32 * s : 32 * s + 32]
        parts[s, :, 32:NZ] = jnp.zeros((16, NZ - 32), jnp.float32)

    def block_copy(dest, origin):
        return pltpu.make_async_remote_copy(
            src_ref=parts.at[dest],
            dst_ref=blocks.at[origin],
            send_sem=blk_send.at[dest],
            recv_sem=blk_recv.at[origin],
            device_id=(dest, me),
            device_id_type=MESH,
        )

    @pl.loop(1, SECTORS)
    def _(off):
        block_copy(lax.rem(sec + off, SECTORS), sec).start()

    blocks[sec] = parts[sec]

    @pl.loop(1, SECTORS)
    def _(off):
        block_copy(sec, lax.rem(sec + off, SECTORS)).wait_recv()

    block = blocks[0]
    for s in range(1, SECTORS):
        block = block + blocks[s]
    out[...] = jnp.transpose(block)[0:32, :]

    for index in range(len(PIECES)):

        @pl.loop(1, GROUPS)
        def _(off, index=index):
            piece_copy(index, peer(off), me).wait_send()

    @pl.loop(1, GROUPS)
    def _(off):
        lam_copy(peer(off), me).wait_send()
        sum_copy(peer(off), me).wait_send()

    @pl.loop(1, SECTORS)
    def _(off):
        block_copy(lax.rem(sec + off, SECTORS), sec).wait_send()


def on_device(modes, thickness, stiff_taps, mass_taps, eigenvalues):
    src = modes.transpose(2, 1, 3, 0, 4).reshape(PLANES, ALL_ROWS, 16, NZ)
    smem = pl.BlockSpec(memory_space=pltpu.SMEM)
    vmem = pl.BlockSpec(memory_space=pltpu.VMEM)
    dma = pltpu.SemaphoreType.DMA
    f32 = jnp.float32
    return pl.pallas_call(
        kernel,
        out_shape=jax.ShapeDtypeStruct((32, 16), f32),
        in_specs=[pl.BlockSpec(memory_space=pl.ANY), vmem, smem, smem, smem],
        out_specs=vmem,
        scratch_shapes=[
            pltpu.VMEM((PLANES + 1, GROUPS, ROWS + 1, 16, NZ), jnp.bfloat16),
            pltpu.VMEM((3, ROWS, MODES, 2 * NZ), f32),
            pltpu.VMEM((2, 3, ROWS, 3 * NZ, 2 * NZ), jnp.bfloat16),
            pltpu.VMEM((3 * NZ, 2 * NZ), jnp.bfloat16),
            pltpu.VMEM((3, 3, 2, 3, ROWS, NZ), f32),
            pltpu.VMEM((11, 16, NZ), jnp.bfloat16),
            pltpu.VMEM((NY, NZ), f32),
            pltpu.VMEM((3, PLANES + 1, 32, NZ), f32),
            pltpu.VMEM((GROUPS, 16, NZ), f32),
            pltpu.VMEM((GROUPS, 16, MODES), f32),
            pltpu.VMEM((GROUPS, 16, MODES), f32),
            pltpu.VMEM((SECTORS, 16, NZ), f32),
            pltpu.VMEM((SECTORS, 16, NZ), f32),
            dma((len(PIECES), GROUPS)),
            dma((len(PIECES), GROUPS)),
            dma((PLANES,)),
            dma((2,)),
            dma((2,)),
            dma((GROUPS,)),
            dma((GROUPS,)),
            dma((GROUPS,)),
            dma((GROUPS,)),
            dma((SECTORS,)),
            dma((SECTORS,)),
        ],
        compiler_params=pltpu.CompilerParams(
            collective_id=0, has_side_effects=True, vmem_limit_bytes=42 * 2**20
        ),
    )(src, thickness, stiff_taps, mass_taps, eigenvalues)


def solution(mesh):
    in_specs = (P("mode", None, "sector", None, None), P("sector", None, None), P(), P(), P("mode"))
    return jax.shard_map(
        on_device, mesh=mesh, in_specs=in_specs, out_specs=P("sector", "mode"), check_vma=False
    )
```
